32 devices in a mesh: wide: 8 (over y, x, core), narrow: 4 (over z).
Axes of the slice: x: 2, y: 2, z: 4, core: 2. Of those that a mesh axis runs over, the one named last changes fastest.
Arguments:
- batch_index: int32 [256], P('narrow'), may hold values from 0 to 255
- train_features: float32 [1024, 1024], P('narrow'), may hold values from -6 to 6
- train_labels: float32 [1024, 1000], P('narrow'), may hold values from -12 to 12
- centers: float32 [8192, 1024], P(('wide', 'narrow')), may hold values from -6 to 6
- weights: float32 [8192, 1000], P(('wide', 'narrow')), may hold values from -6 to 6
Outputs:
- new_weights: float32 [8192, 1000], P(('wide', 'narrow'))
- residual: float32 [256, 1000], P('narrow')
The draws below stay inside these ranges and needn't reach their ends.
Inputs may be any that keep to these rules, and one draw needn't show every extreme that they name: `batch_index`: entry i names a row of the training shard held by narrow index i // 64.
All inputs are finite; a program needn't handle non-finite values.
Results may differ from the reference program's by a relative error of at most 0.0001.
Values sent between devices are 32-bit elements; how exact they have to be, the bound alone decides.
A program may use at most 64 MiB of HBM per device.

```python
import math
import jax
import jax.numpy as jnp
from jax import lax

D = 1024
L = 1000
M_DEV = 256
BLOCK = 64
TRAIN_DEV = 256
BATCH = 256
CENTERS = 8192
TRAIN = 1024
N_WIDE = 8
N_NARROW = 4


def shaped_rows(key, offset, row_count):
    own_key = jax.random.fold_in(key, offset)
    entry_key, norm_key = jax.random.split(own_key)
    sample = jax.random.normal(entry_key, (row_count, D), jnp.float32)
    square = jax.random.uniform(norm_key, (row_count, 1), jnp.float32, 0.85, 1.15)
    length = jnp.sqrt(jnp.sum(sample * sample, axis=1, keepdims=True))
    return jnp.clip(sample * jnp.sqrt(square * D) / length, -6.0, 6.0)


def draw_train_features(key, part):
    return shaped_rows(key, 11, TRAIN)


def draw_centers(key, part):
    return shaped_rows(key, 23, CENTERS)


def with_ends(values, rng, low, high):
    extent = values.shape
    index_at = [jax.random.randint(jax.random.fold_in(rng, axis), (), 0, extent[axis]) for axis in range(len(extent))]
    values = values.at[tuple(index_at)].set(low)
    longest = extent.index(max(extent))
    index_at[longest] = (index_at[longest] + 1) % extent[longest]
    return values.at[tuple(index_at)].set(high)


def shard_levels(rng, dims, shards, least, top_value):
    loudness = 1.0
    for position, blocks in shards:
        draws = jax.random.uniform(jax.random.fold_in(jax.random.fold_in(rng, 6), position), (blocks,), jnp.float32, least / len(shards), top_value / len(shards))
        loudness = loudness * jnp.repeat(jnp.exp(draws), dims[position] // blocks).reshape((-1,) + (1,) * (len(dims) - 1 - position))
    return loudness


def centred(key, dims, deviation, reach, shards=(), kind=jnp.bfloat16):
    drawn = jax.random.normal(key, dims, jnp.float32) * deviation
    if len(shards) > 0:
        drawn = shard_levels(key, dims, shards, -0.22, 0.18) * drawn
    return jnp.clip(drawn, min=-reach, max=reach).astype(kind)


def setup_inputs(seed: int = 0) -> dict:
    arg_keys = jax.random.split(jax.random.key(seed), 6)
    return {
        "batch_index": with_ends(jax.random.randint(arg_keys[0], (BATCH,), 0, TRAIN_DEV), jax.random.fold_in(arg_keys[0], 1), 0, TRAIN_DEV - 1).astype(jnp.int32),
        "train_features": draw_train_features(jax.random.fold_in(arg_keys[5], 71), 0),
        "train_labels": centred(arg_keys[2], (TRAIN, L), 2.0, 12.0, ((0, 4),), jnp.float32),
        "centers": draw_centers(jax.random.fold_in(arg_keys[5], 71), 0),
        "weights": centred(arg_keys[4], (CENTERS, L), 1.0, 6.0, ((0, 32),), jnp.float32),
    }


step_size = 1.0

def kernel_block(rows, centers_blk):
    inner = jnp.dot(rows, centers_blk.T, precision=lax.Precision.HIGHEST, preferred_element_type=jnp.float32)
    row_sq = lax.optimization_barrier(jnp.sum(rows * rows, axis=1))
    center_sq = lax.optimization_barrier(jnp.sum(centers_blk * centers_blk, axis=1))
    return jnp.exp((2.0 * rows.shape[1] - row_sq[:, None] - center_sq[None, :] + 2.0 * inner) / 128.0)

def reference(batch_index, train_features, train_labels, centers, weights):
    picks = jnp.arange(BATCH, dtype=jnp.int32) // BLOCK * TRAIN_DEV + batch_index.astype(jnp.int32)
    rows = jnp.take(train_features, picks, axis=0)
    targets = jnp.take(train_labels, picks, axis=0)
    groups = N_WIDE * N_NARROW
    center_blocks = centers.reshape(groups, M_DEV, D)
    weight_blocks = weights.reshape(groups, M_DEV, L)

    def accumulate(total, pair):
        kern = kernel_block(rows, pair[0])
        return (total + jnp.dot(kern, pair[1], precision=lax.Precision.HIGHEST, preferred_element_type=jnp.float32), None)
    partial_value, _ = lax.scan(accumulate, jnp.zeros((BATCH, L), jnp.float32), (center_blocks, weight_blocks))
    residual = partial_value * (1.0 / math.sqrt(CENTERS)) - targets

    def update(pair):
        kern = kernel_block(rows, pair[0])
        delta = lax.dot_general(kern, residual, (((0,), (0,)), ((), ())), precision=lax.Precision.HIGHEST, preferred_element_type=jnp.float32)
        return pair[1] - step_size / BATCH * delta
    new_weights = lax.map(update, (center_blocks, weight_blocks)).reshape(CENTERS, L)
    return (new_weights, residual)
```

```python
import functools
import math

import jax
import jax.numpy as jnp
from jax import lax
from jax.experimental import pallas as pl
from jax.experimental.pallas import tpu as pltpu
from jax.sharding import PartitionSpec as P

step_size = 1.0
MESH = pl.DeviceIdType.MESH
HIGHEST = lax.Precision.HIGHEST
SUB = 8
LANES = 128


def dot(a, b, dims):
    return lax.dot_general(
        a, b, (dims, ((), ())), precision=HIGHEST, preferred_element_type=jnp.float32
    )


def split(x, count):
    terms = []
    for _ in range(count):
        terms.append(x.astype(jnp.bfloat16))
        x = x - terms[-1].astype(jnp.float32)
    return terms


def split_dot(a, b):
    held = a[0].shape[0]
    orders = [[] for _ in a]
    for i, right in enumerate(b):
        left = a[: len(a) - i]
        out = lax.dot_general(
            jnp.concatenate(left, axis=0), right, (((1,), (1,)), ((), ())),
            preferred_element_type=jnp.float32,
        )
        for j in range(len(left)):
            orders[i + j].append(out[j * held : (j + 1) * held])
    total = 0.0
    for terms in orders[::-1]:
        total = total + sum(terms)
    return total


def flip(q, k):
    out = q
    for b in range(k.bit_length()):
        if k >> b & 1:
            out = out + 2**b * (1 - 2 * ((q // 2**b) % 2))
    return out


def by_distance(n, narrow):
    picks = []
    for p in range(1, narrow):
        m = 0
        for i in range(narrow):
            near = sorted(range(narrow), key=lambda j: abs(j - i))
            m = m + jnp.where(n == i, near[p], 0)
        picks.append(m)
    return picks


def step_kernel(
    wide, narrow, count, index_ref, tf_hbm, lab_hbm, cen_hbm, wgt_hbm, delta_hbm, res_hbm,
    tf, lab, cen, wgt, cen_terms, wgt_terms, rows, kern, away, part, got, zgot, resid, tgt, acc, load_sem,
    zrow_s, zrow_r, row_s, row_r, pair_s, pair_r, kern_s, kern_r, red_s, red_r, zred_s, zred_r,
    zag_s, zag_r, ag_s, ag_r, core_s, core_r, out_sem,
):
    w, n = lax.axis_index("wide"), lax.axis_index("narrow")
    plane = wide // 2
    c, q = w % 2, w // 2
    piece, features = rows.shape[2], rows.shape[3]
    half, outputs = plane * piece, acc.shape[0]
    partner = (w + 1 - 2 * c, n)
    hops = list(range(plane - 1, 0, -1))
    peer = {k: (flip(q, k) * 2 + c, n) for k in hops}
    others = by_distance(n, narrow)

    loads = [
        pltpu.make_async_copy(src, dst, load_sem.at[i])
        for i, (src, dst) in enumerate(((tf_hbm, tf), (cen_hbm, cen.at[0]), (wgt_hbm, wgt.at[0]), (lab_hbm, lab)))
    ]
    for load in loads:
        load.start()
    barrier = pltpu.get_barrier_semaphore()
    greeted = [(w, m) for m in others] + [peer[k] for k in hops] + [partner]
    for p in greeted:
        pl.semaphore_signal(barrier, inc=1, device_id=p, device_id_type=MESH)

    def copy(src, dst, ssem, rsem, to):
        return pltpu.make_async_remote_copy(
            src_ref=src, dst_ref=dst, send_sem=ssem, recv_sem=rsem, device_id=to, device_id_type=MESH
        )

    sent = []

    def send(*args):
        sent.append(copy(*args))
        sent[-1].start()

    loads[0].wait()
    first = c * half
    for g in range(plane):
        picked = [tf[pl.ds(index_ref[first + g * piece + i], 1), :] for i in range(piece)]
        rows[n, g] = jnp.concatenate(picked, axis=0)
    pl.semaphore_wait(barrier, len(greeted))

    for m in others:
        send(rows.at[n, q], rows.at[n, q], zrow_s.at[m], zrow_r.at[n], (w, m))
    loads[1].wait()
    send(cen.at[0], cen.at[1], pair_s.at[0], pair_r.at[0], partner)
    loads[2].wait()
    send(wgt.at[0], wgt.at[1], pair_s.at[1], pair_r.at[1], partner)

    def squares(o):
        centers = cen[o]
        for i, term in enumerate(split(centers, 3)):
            cen_terms[o, i] = term
        sq = centers * centers
        narrowed = sum(sq[:, j * LANES : (j + 1) * LANES] for j in range(features // LANES))
        return dot(jnp.ones((SUB, LANES), jnp.float32), narrowed, ((1,), (1,)))[0:1, :]

    def weigh(o):
        for i, term in enumerate(split(wgt[o], 2)):
            wgt_terms[o, i] = term

    def spread_rows(m):
        copy(rows.at[m, q], rows.at[m, q], zrow_s.at[m], zrow_r.at[m], partner).wait_recv()
        for k in hops:
            send(rows.at[m, q], rows.at[m, q], row_s.at[k, m], row_r.at[k, m], peer[k])

    center_sq = []

    def kernels(m, o, terms, sq):
        inner = split_dot(terms, [cen_terms[o, i] for i in range(3)])
        return jnp.exp((2.0 * features - sq - center_sq[o] + 2.0 * inner) / 128.0)

    def block_rows(m):
        mine = rows[m].reshape(half, features)
        return split(mine, 3), jnp.sum(mine * mine, axis=1, keepdims=True)

    def predict(o, value):
        return split_dot(split(value, 2), [wgt_terms[o, i] for i in range(2)])

    def reduce_send(m, total):
        part[m] = total.reshape(plane, piece, outputs)
        for k in hops:
            send(part.at[m, flip(q, k)], got.at[k, m], red_s.at[k, m], red_r.at[k, m], peer[k])
        send(away.at[m], kern.at[m, c], kern_s.at[m], kern_r.at[m], partner)

    def finish(m, terms, sq):
        value = kernels(m, 0, terms, sq)
        kern[m, c] = value
        total = predict(0, value)
        value = kernels(m, 1, terms, sq)
        away[m] = value
        reduce_send(m, total + predict(1, value))

    terms, sq = block_rows(n)
    center_sq.append(squares(0))
    weigh(0)
    value = kernels(n, 0, terms, sq)
    kern[n, c] = value
    total = predict(0, value)
    spread_rows(others[0])
    copy(cen.at[0], cen.at[1], pair_s.at[0], pair_r.at[0], partner).wait_recv()
    center_sq.append(squares(1))
    for m in others[1:]:
        spread_rows(m)
    copy(wgt.at[0], wgt.at[1], pair_s.at[1], pair_r.at[1], partner).wait_recv()
    weigh(1)
    value = kernels(n, 1, terms, sq)
    away[n] = value
    reduce_send(n, total + predict(1, value))

    loads[3].wait()
    own = first + q * piece
    column = lax.broadcasted_iota(jnp.int32, (1, lab.shape[1]), 1)
    chosen = [jnp.where(column == index_ref[own + i], 1.0, 0.0) for i in range(piece)]
    tgt[...] = dot(jnp.concatenate(chosen, axis=0), lab[...], ((1,), (1,)))

    def reduced(m):
        total = part[m, q]
        for k in hops[::-1]:
            copy(part.at[m, q], got.at[k, m], red_s.at[k, m], red_r.at[k, m], partner).wait_recv()
            total = total + got[k, m]
        return total

    def pass_on(m):
        part[m, q] = reduced(m)
        send(part.at[m, q], zgot.at[n], zred_s.at[m], zred_r.at[n], (w, m))

    for p, m in enumerate(others):
        for k in hops[::-1]:
            copy(rows.at[m, q], rows.at[m, flip(q, k)], row_s.at[k, m], row_r.at[k, m], partner).wait_recv()
        finish(m, *block_rows(m))
        if p > 0:
            pass_on(others[p - 1])
    total = reduced(n)
    pass_on(others[-1])
    for m in others:
        copy(part.at[m, q], zgot.at[m], zred_s.at[m], zred_r.at[m], partner).wait_recv()
        total = total + zgot[m]
    resid[n, c, q] = total * (1.0 / math.sqrt(count)) - tgt[...]

    def around(m):
        for k in hops:
            send(resid.at[m, c, q], resid.at[m, c, q], ag_s.at[k, m], ag_r.at[k, m], peer[k])

    for m in others:
        send(resid.at[n, c, q], resid.at[n, c, q], zag_s.at[m], zag_r.at[n], (w, m))
    around(n)

    def onward(m):
        copy(resid.at[m, c, q], resid.at[m, c, q], zag_s.at[m], zag_r.at[m], partner).wait_recv()
        around(m)

    def across(m):
        for k in hops[::-1]:
            there = resid.at[m, c, flip(q, k)]
            copy(there, there, ag_s.at[k, m], ag_r.at[k, m], partner).wait_recv()
        send(resid.at[m, c], resid.at[m, c], core_s.at[m], core_r.at[m], partner)

    def terms_of(m):
        copy(resid.at[m, c], resid.at[m, 1 - c], core_s.at[m], core_r.at[m], partner).wait_recv()
        copy(away.at[m], kern.at[m, 1 - c], kern_s.at[m], kern_r.at[m], partner).wait_recv()
        k_hi, k_lo = split(kern[m].reshape(2 * half, kern.shape[3]), 2)
        r_hi, r_lo = split(resid[m].reshape(2 * half, outputs), 2)
        return jnp.concatenate([r_hi, r_hi, r_lo], axis=0), jnp.concatenate([k_hi, k_lo, k_hi], axis=0)

    def contract(r, k):
        return lax.dot_general(r, k, (((0,), (0,)), ((), ())), preferred_element_type=jnp.float32)

    outs = [pltpu.make_async_copy(resid.at[n], res_hbm, out_sem.at[0])]
    order = [n] + others
    for p, m in enumerate(order):
        if p == 0:
            onward(others[0])
            across(n)
            for later in others[1:]:
                onward(later)
        else:
            across(m)
            before = order[p - 1]
            d = contract(*terms_of(before))
            acc[...] = d if p == 1 else acc[...] + d
            if p == 1:
                outs[0].start()
    r, k = terms_of(order[-1])
    cut = 2 * LANES
    for j, at in enumerate(range(0, outputs, cut)):
        span = pl.ds(at, min(cut, outputs - at))
        acc[span, :] = acc[span, :] + contract(r[:, at : at + cut], k)
        outs.append(pltpu.make_async_copy(acc.at[span], delta_hbm.at[span], out_sem.at[1 + j]))
        outs[-1].start()
    for s in sent:
        s.wait_send()
    for s in outs:
        s.wait()


def per_device(batch_index, train_features, train_labels, centers, weights):
    wide, narrow = lax.axis_size("wide"), lax.axis_size("narrow")
    block, features = batch_index.shape[0], centers.shape[1]
    outputs, owned = weights.shape[1], centers.shape[0]
    labels_t, weights_t = train_labels.T, weights.T
    plane, half = wide // 2, block // 2
    piece = half // plane
    f32, dma = jnp.float32, pltpu.SemaphoreType.DMA
    anywhere = pl.BlockSpec(memory_space=pl.ANY)
    each, pairs = dma((narrow,)), dma((plane, narrow))
    delta_t, residual = pl.pallas_call(
        functools.partial(step_kernel, wide, narrow, owned * wide * narrow),
        out_shape=(
            jax.ShapeDtypeStruct((outputs, owned), f32),
            jax.ShapeDtypeStruct((2, plane, piece, outputs), f32),
        ),
        in_specs=[pl.BlockSpec(memory_space=pltpu.SMEM)] + [anywhere] * 4,
        out_specs=(anywhere, anywhere),
        scratch_shapes=[
            pltpu.VMEM(train_features.shape, f32),
            pltpu.VMEM(labels_t.shape, f32),
            pltpu.VMEM((2, *centers.shape), f32),
            pltpu.VMEM((2, *weights_t.shape), f32),
            pltpu.VMEM((2, 3, *centers.shape), jnp.bfloat16),
            pltpu.VMEM((2, 2, *weights_t.shape), jnp.bfloat16),
            pltpu.VMEM((narrow, plane, piece, features), f32),
            pltpu.VMEM((narrow, 2, half, owned), f32),
            pltpu.VMEM((narrow, half, owned), f32),
            pltpu.VMEM((narrow, plane, piece, outputs), f32),
            pltpu.VMEM((plane, narrow, piece, outputs), f32),
            pltpu.VMEM((narrow, piece, outputs), f32),
            pltpu.VMEM((narrow, 2, plane, piece, outputs), f32),
            pltpu.VMEM((piece, outputs), f32),
            pltpu.VMEM((outputs, owned), f32),
            dma((4,)),
            each, each, pairs, pairs,
            dma((2,)), dma((2,)),
            each, each, pairs, pairs,
            each, each,
            each, each, pairs, pairs,
            each, each,
            dma((2 + outputs // (2 * LANES),)),
        ],
        compiler_params=pltpu.CompilerParams(
            collective_id=0, has_side_effects=True, vmem_limit_bytes=60 * 2**20
        ),
    )(batch_index, train_features, labels_t, centers, weights_t)
    new_weights = weights - step_size / (narrow * block) * delta_t.T
    return new_weights, residual.reshape(block, outputs)


def solution(mesh):
    in_specs = (
        P("narrow"),
        P("narrow", None),
        P("narrow", None),
        P(("wide", "narrow"), None),
        P(("wide", "narrow"), None),
    )
    out_specs = (P(("wide", "narrow"), None), P("narrow", None))
    return jax.shard_map(
        per_device, mesh=mesh, in_specs=in_specs, out_specs=out_specs, check_vma=False
    )
```
